32 devices in a mesh: group: 8 (over z, core), dp: 4 (over y, x).
Axes of the slice: x: 2, y: 2, z: 4, core: 2. Of those that a mesh axis runs over, the one named last changes fastest.
Arguments:
- resp_q: bfloat16 [8, 1024, 4096], P('group', 'dp'), may hold values from -410 to 410
- resp_k: bfloat16 [8, 1024, 4096], P('group', 'dp'), may hold values from -410 to 410
- resp_v: bfloat16 [8, 1024, 4096], P('group', 'dp'), may hold values from -6 to 6
- prompt_k: bfloat16 [8, 512, 4096], P('group', 'dp'), may hold values from -410 to 410
- prompt_v: bfloat16 [8, 512, 4096], P('group', 'dp'), may hold values from -6 to 6
- prompt_len: int32 [8], P('group'), may hold values from 128 to 512
- resp_len: int32 [8, 4], P('group', 'dp'), may hold values from 1 to 256, as said below
- assign: int32 [8, 8], P('group', 'dp'), may hold values from 0 to 15, as said below
- rewards: float32 [8, 4], P('group', 'dp'), may hold values from -18 to 18
- feat_q: bfloat16 [32, 128, 128], replicated, may hold values from -1 to 1
- feat_k: bfloat16 [32, 128, 128], replicated, may hold values from -1 to 1
Outputs:
- attn_out: bfloat16 [8, 512, 4096], P('group', 'dp')
- token_adv: float32 [8, 512], P('group', 'dp')
The draws below stay inside these ranges and needn't reach their ends.
Inputs may be any that keep to these rules, and one draw needn't show every extreme that they name: Response r of a prompt has ceil(resp_len / 64) live blocks; these counts sum to 2 * 4 over a prompt's responses, and one response of every prompt has 4 blocks. `assign`: entry d * 2 + j names the block r * 4 + c (block c of response r) whose outputs go to slot j of device d of dp. Every live block of the prompt is named exactly once, and the 2 slots of one device name blocks of different responses.
All inputs are finite; a program needn't handle non-finite values.
Results may differ from the reference program's by a relative error of at most 0.0085.
Values may be sent and summed in bfloat16 or wider, within the bound.
A program may use at most 128 MiB of HBM per device.

```python
import jax
import jax.numpy as jnp
from jax import lax

H = 32
DH = 128
FH = 128
BLK = 64
MAXC = 4
CAP = 2
PT_DEV = 128
PROMPTS = 8
RESP = 4


def heavy_draw(key, rows, salt):
    stream = jax.random.fold_in(key, salt)
    first_key = jax.random.fold_in(stream, 0)
    extent = (PROMPTS, rows, H * DH)
    sample = jnp.clip(jax.random.normal(first_key, extent, jnp.float32), -6.0, 6.0)
    return sample.astype(jnp.bfloat16)


def draw_resp_q(key, part):
    return heavy_draw(key, RESP * MAXC * BLK, 101)


def draw_resp_k(key, part):
    return heavy_draw(key, RESP * MAXC * BLK, 202)


def draw_prompt_k(key, part):
    return heavy_draw(key, RESP * PT_DEV, 303)


def draw_rewards(key, part):
    stream = jax.random.fold_in(key, 404)
    first_key = jax.random.fold_in(stream, 0)
    rising = 1.0 + 2.0 * jnp.arange(PROMPTS, dtype=jnp.float32)[:, None] / (PROMPTS - 1)
    sample = jnp.clip(jax.random.normal(first_key, (PROMPTS, RESP), jnp.float32), -6.0, 6.0) * rising
    return sample


def stretch_plan(key):

    def per_prompt(prompt_key):
        slot_key, lead_key, tail_key, order_key, device_key = jax.random.split(prompt_key, 5)
        slots = RESP * (MAXC - 1)
        counter = jnp.arange(slots, dtype=jnp.int32)
        ranking = jax.random.randint(slot_key, (slots,), 0, 1 << 20).astype(jnp.int32) * slots + counter
        leader = jax.random.randint(lead_key, (), 0, RESP).astype(jnp.int32)
        owner = counter // (MAXC - 1)
        ranking = jnp.where(owner == leader, (1 << 20) * slots + counter, ranking)
        ordering = jnp.argsort(-ranking)
        chosen = jnp.zeros((slots,), jnp.int32).at[ordering[:RESP * (CAP - 1)]].set(1)
        blocks = 1 + chosen.reshape(RESP, MAXC - 1).sum(axis=1)
        tails = jax.random.randint(tail_key, (RESP,), 1, BLK + 1).astype(jnp.int32)
        tokens = (blocks - 1) * BLK + tails
        index_row = jnp.arange(RESP, dtype=jnp.int32)
        sigma = jnp.argsort(jax.random.randint(order_key, (RESP,), 0, 1 << 20).astype(jnp.int32) * RESP + index_row)
        devperm = jnp.argsort(jax.random.randint(device_key, (RESP,), 0, 1 << 20).astype(jnp.int32) * RESP + index_row)
        ordered = blocks[sigma]
        starts = jnp.cumsum(ordered) - ordered
        stream_index = jnp.arange(RESP * CAP, dtype=jnp.int32)
        located = jnp.sum((starts[None, :] <= stream_index[:, None]).astype(jnp.int32), axis=1) - 1
        response = sigma[located]
        within = stream_index - starts[located]
        target = devperm[stream_index % RESP] * CAP + stream_index // RESP
        table = jnp.zeros((RESP * CAP,), jnp.int32).at[target].set((response * MAXC + within).astype(jnp.int32))
        return (tokens.astype(jnp.int32), table)
    prompt_keys = jax.random.split(jax.random.fold_in(key, 505), PROMPTS)
    return jax.vmap(per_prompt)(prompt_keys)


def draw_resp_len(key, part):
    return stretch_plan(key)[0]


def draw_assign(key, part):
    return stretch_plan(key)[1]


def set_ends(result, stream_key, least, top_value):
    longest = result.shape.index(max(result.shape))
    spots = []
    for shift in (0, 1):
        where = [jax.random.randint(jax.random.fold_in(stream_key, axis), (), 0, length) for axis, length in enumerate(result.shape)]
        where[longest] = (where[longest] + shift) % result.shape[longest]
        spots.append(tuple(where))
    return result.at[spots[0]].set(least).at[spots[1]].set(top_value)


def steps_of(own_key, shape, shards, least, largest):
    def one(position, parts):
        heights = jax.random.uniform(jax.random.fold_in(jax.random.fold_in(own_key, 6), position), (parts,), jnp.float32, least / len(shards), largest / len(shards))
        return jnp.repeat(jnp.exp(heights), shape[position] // parts).reshape((-1,) + (1,) * (len(shape) - position - 1))

    level = one(*shards[0])
    for cut in shards[1:]:
        level = level * one(*cut)
    return level


def bell_draw(stream_key, dims, scale, reach, cuts=(), held_as=jnp.bfloat16):
    array = scale * jax.random.normal(stream_key, dims, jnp.float32)
    if cuts:
        array = array * steps_of(stream_key, dims, cuts, -0.22, 0.18)
    return jnp.clip(array, -reach, reach).astype(held_as)


def setup_inputs(seed: int = 0) -> dict:
    splits = jax.random.split(jax.random.key(seed), 12)
    resp_q = draw_resp_q(jax.random.fold_in(splits[11], 71), 0)
    resp_k = draw_resp_k(jax.random.fold_in(splits[11], 71), 0)
    resp_v = bell_draw(splits[2], (PROMPTS, RESP * MAXC * BLK, H * DH), 1.0, 6.0, ((0, 8), (1, 4)))
    prompt_k = draw_prompt_k(jax.random.fold_in(splits[11], 71), 0)
    prompt_v = bell_draw(splits[4], (PROMPTS, RESP * PT_DEV, H * DH), 1.0, 6.0, ((0, 8), (1, 4)))
    prompt_len = set_ends(jax.random.randint(splits[5], (PROMPTS,), RESP * PT_DEV // 4, RESP * PT_DEV + 1), jax.random.fold_in(splits[5], 1), RESP * PT_DEV // 4, RESP * PT_DEV).astype(jnp.int32)
    resp_len = draw_resp_len(jax.random.fold_in(splits[11], 71), 0)
    assign = draw_assign(jax.random.fold_in(splits[11], 71), 0)
    rewards = draw_rewards(jax.random.fold_in(splits[11], 71), 0)
    feat_q = bell_draw(splits[9], (H, DH, FH), (DH // 4) ** -0.5, 1.0)
    feat_k = bell_draw(splits[10], (H, DH, FH), (DH // 4) ** -0.5, 1.0)
    return dict(resp_q=resp_q, resp_k=resp_k, resp_v=resp_v, prompt_k=prompt_k, prompt_v=prompt_v, prompt_len=prompt_len, resp_len=resp_len, assign=assign, rewards=rewards, feat_q=feat_q, feat_k=feat_k)


def features(rows, weights):
    logits = jnp.einsum('thd,hdf->thf', rows.astype(jnp.float32), weights.astype(jnp.float32), precision=lax.Precision.HIGHEST)
    return jnp.concatenate([jax.nn.softmax(logits, axis=-1), jax.nn.softmax(-logits, axis=-1)], axis=-1).astype(jnp.bfloat16)

def reference(resp_q, resp_k, resp_v, prompt_k, prompt_v, prompt_len, resp_len, assign, rewards, feat_q, feat_k):
    head_count = feat_q.shape[0]
    head_width = feat_q.shape[1]
    length = MAXC * BLK
    prompt_rows = prompt_k.shape[1]
    causal = jnp.arange(length)[:, None] >= jnp.arange(length)[None, :]
    highest = lax.Precision.HIGHEST

    def per_prompt(operands):
        queries, key_rows, value_rows, prompt_keys, prompt_values, limit, lengths, slot_ids = operands
        prompt_feat = features(prompt_keys.reshape(prompt_rows, head_count, head_width), feat_k)
        keep = jnp.arange(prompt_rows) < limit
        masked = jnp.where(keep[:, None, None], prompt_feat.astype(jnp.float32), jnp.float32(0.0))
        kv_state = jnp.einsum('shf,she->hfe', masked, prompt_values.reshape(prompt_rows, head_count, head_width).astype(jnp.float32), precision=highest).astype(jnp.bfloat16)
        key_total = lax.optimization_barrier(jnp.sum(masked, axis=0)).astype(jnp.bfloat16)

        def per_response(items):
            query_rows, key_block, value_block, size = items
            query_feat = features(query_rows.reshape(length, head_count, head_width), feat_q).astype(jnp.float32)
            key_feat = features(key_block.reshape(length, head_count, head_width), feat_k).astype(jnp.float32)
            prompt_num = jnp.einsum('thf,hfe->the', query_feat, kv_state.astype(jnp.float32), precision=highest).astype(jnp.bfloat16)
            prompt_den = jnp.einsum('thf,hf->th', query_feat, key_total.astype(jnp.float32), precision=highest).astype(jnp.bfloat16)
            scores = jnp.einsum('thf,shf->hts', query_feat, key_feat, precision=highest)
            scores = jnp.where(causal[None], scores, jnp.float32(0.0))
            intra_den = lax.optimization_barrier(jnp.sum(scores, axis=-1))
            rounded = lax.optimization_barrier(scores.astype(jnp.bfloat16)).astype(jnp.float32)
            values_f = value_block.reshape(length, head_count, head_width).astype(jnp.float32)
            intra_num = jnp.einsum('hts,she->the', rounded, values_f, precision=highest)
            combined = (prompt_num.astype(jnp.float32) + intra_num) / (prompt_den.astype(jnp.float32) + intra_den.T)[:, :, None]
            live_rows = jnp.arange(length) < size
            combined = jnp.where(live_rows[:, None, None], combined, jnp.float32(0.0))
            return combined.astype(jnp.bfloat16).reshape(MAXC, BLK, head_count * head_width)
        outputs = lax.map(per_response, (queries.reshape(RESP, length, head_count * head_width), key_rows.reshape(RESP, length, head_count * head_width), value_rows.reshape(RESP, length, head_count * head_width), lengths))
        flat = outputs.reshape(RESP * MAXC, BLK, head_count * head_width)
        return jnp.take(flat, slot_ids.astype(jnp.int32), axis=0).reshape(RESP * CAP * BLK, head_count * head_width)
    attended = lax.map(per_prompt, (resp_q, resp_k, resp_v, prompt_k, prompt_v, prompt_len, resp_len, assign))
    centred = rewards - lax.optimization_barrier(jnp.mean(rewards, axis=1, keepdims=True))
    spread = jnp.mean(centred * centred)
    advantage = centred / jnp.sqrt(spread + 1e-06)
    responses = (assign // MAXC).astype(jnp.int32)
    pieces = (assign % MAXC).astype(jnp.int32)
    slot_adv = jnp.take_along_axis(advantage, responses, axis=1)
    slot_len = jnp.take_along_axis(resp_len, responses, axis=1)
    positions = pieces[:, :, None] * BLK + jnp.arange(BLK, dtype=jnp.int32)[None, None, :]
    token_adv = jnp.where(positions < slot_len[:, :, None], slot_adv[:, :, None], jnp.float32(0.0))
    return (attended, token_adv.reshape(rewards.shape[0], RESP * CAP * BLK))
```

```python
import functools

import jax
import jax.numpy as jnp
from jax import lax
from jax.experimental import pallas as pl
from jax.experimental.pallas import tpu as pltpu
from jax.sharding import PartitionSpec as P

BLK = 64
MESH = pl.DeviceIdType.MESH
NT = (((1,), (1,)), ((), ()))
NN = (((1,), (0,)), ((), ()))
F32 = jnp.float32
BF16 = jnp.bfloat16


def dot(a, b, dims=NN):
    return lax.dot_general(a, b, dims, preferred_element_type=F32)


def features(rows, weights, ones_blocks):
    logits = dot(rows, weights)
    top = jnp.max(logits, axis=-1, keepdims=True)
    low = jnp.min(logits, axis=-1, keepdims=True)
    both = jnp.concatenate([jnp.exp(logits - top), jnp.exp(low - logits)], axis=1)
    sums = dot(both.astype(BF16), ones_blocks)
    return (both * (1.0 / sums)).astype(BF16)


def kernel(
    n, groups, heads, chunks,
    plen, rlen, slots_sm, rew_sm, q_hbm, k_hbm, v_hbm, pk_hbm, pv_hbm, fq_hbm, fk_hbm,
    out_ref, adv_ref,
    qs, ks, vs, fqs, fks, kbuf, vbuf, state, totals, phq, inum, ostage, orecv,
    tinfo, trew, tsm, gsum,
    load_sem, self_sem, kv_send, kv_recv, st_send, st_recv, o_send, o_recv,
    i_send, i_recv, g_send, g_recv, sm_sem,
):
    me = lax.axis_index("dp")
    grp = lax.axis_index("group")
    rows = qs.shape[0]
    width = fqs.shape[2]
    pieces = rows // BLK
    slot_count = slots_sm.shape[1]
    own = heads // n
    per = own // chunks
    prows = pk_hbm.shape[1]

    def peer(i):
        return lax.rem(me + i, n)

    def source(i):
        return lax.rem(me + (n - i), n)

    loads = [
        pltpu.make_async_copy(src, dst, load_sem.at[i])
        for i, (src, dst) in enumerate(
            [(fq_hbm, fqs), (fk_hbm, fks), (q_hbm.at[0], qs), (k_hbm.at[0], ks), (v_hbm.at[0], vs)]
        )
    ]

    lane = lax.broadcasted_iota(jnp.int32, (8, 128), 1)
    info = jnp.where(lane == slot_count, rlen[0, 0], 0)
    for j in range(slot_count):
        info = jnp.where(lane == j, slots_sm[0, j], info)
    tinfo[me] = info
    trew[me] = jnp.full((8, 128), rew_sm[0, 0], F32)

    barrier = pltpu.get_barrier_semaphore()
    for i in range(1, n):
        pl.semaphore_signal(barrier, inc=1, device_id={"dp": peer(i)}, device_id_type=MESH)
    for i in range(1, groups):
        pl.semaphore_signal(
            barrier, inc=1, device_id={"group": lax.rem(grp + i, groups)}, device_id_type=MESH
        )
    for copy in loads:
        copy.start()
    pl.semaphore_wait(barrier, n + groups - 2)

    def remote(src, dst, send, recv, axis, target):
        return pltpu.make_async_remote_copy(
            src_ref=src, dst_ref=dst, send_sem=send, recv_sem=recv,
            device_id={axis: target}, device_id_type=MESH,
        )

    def kv_cols(owner, c):
        return pl.ds(pl.multiple_of((owner * own + c * per) * width, 128), per * width)

    def kv_copies(c, i):
        result = []
        for a, (hbm, buf) in enumerate([(pk_hbm, kbuf), (pv_hbm, vbuf)]):
            src = hbm.at[0, :, kv_cols(peer(i), c)]
            dst = buf.at[c, me]
            if i == 0:
                result.append(pltpu.make_async_copy(src, dst, self_sem.at[c, a]))
            else:
                result.append(
                    remote(src, dst, kv_send.at[c, a, i], kv_recv.at[c, a, i], "dp", peer(i))
                )
        return result

    def info_copies(i):
        return [
            remote(tinfo.at[me], tinfo.at[me], i_send.at[0, i], i_recv.at[0, i], "dp", peer(i)),
            remote(trew.at[me], trew.at[me], i_send.at[1, i], i_recv.at[1, i], "dp", peer(i)),
        ]

    def group_copy(i):
        return remote(
            gsum.at[grp], gsum.at[grp], g_send.at[i], g_recv.at[i], "group",
            lax.rem(grp + i, groups),
        )

    def state_copies(c, i):
        return [
            remote(
                state.at[me, c], state.at[me, c], st_send.at[c, 0, i], st_recv.at[c, 0, i],
                "dp", peer(i),
            ),
            remote(
                totals.at[me, c], totals.at[me, c], st_send.at[c, 1, i], st_recv.at[c, 1, i],
                "dp", peer(i),
            ),
        ]

    def out_cols(step):
        return pl.ds(pl.multiple_of(source(step) * own * width, 128), own * width)

    def out_copy(step, i):
        cols = out_cols(step)
        return remote(
            ostage.at[i - 1, :, cols], orecv.at[me, :, cols], o_send.at[step, i],
            o_recv.at[step, i], "dp", peer(i),
        )

    for i in range(1, n):
        for copy in info_copies(i):
            copy.start()
    for c in range(chunks):
        for i in [*range(1, n), 0]:
            for copy in kv_copies(c, i):
                copy.start()

    feat = fqs.shape[2]
    left = lax.broadcasted_iota(jnp.int32, (2 * feat, 2 * feat), 0) < feat
    upper = lax.broadcasted_iota(jnp.int32, (2 * feat, 2 * feat), 1) < feat
    ones_blocks = jnp.where(left == upper, 1.0, 0.0).astype(BF16)

    for copy in loads:
        copy.wait()

    def intra_head(h):
        cols = pl.ds(pl.multiple_of(h * width, 128), width)
        qf = features(qs[:, cols], fqs[h], ones_blocks)
        kf = features(ks[:, cols], fks[h], ones_blocks)
        phq[h] = qf
        scores = dot(qf, kf, NT)
        causal = lax.broadcasted_iota(jnp.int32, (rows, rows), 0) >= lax.broadcasted_iota(
            jnp.int32, (rows, rows), 1
        )
        weight = jnp.where(causal, scores, 0.0).astype(BF16)
        value = jnp.concatenate([vs[:, cols], jnp.ones((rows, width), BF16)], axis=1)
        inum[h] = dot(weight, value)

    def intra(first, last):
        def step(t, carry):
            intra_head(first + 2 * t)
            intra_head(first + 2 * t + 1)
            return carry

        lax.fori_loop(0, (last - first) // 2, step, 0)

    def states(c):
        for i in range(n):
            for copy in kv_copies(c, i):
                copy.wait() if i == 0 else copy.wait_recv()
        keep = lax.broadcasted_iota(jnp.int32, (n * prows, 2 * feat), 0) < plen[0]
        line = lax.broadcasted_iota(jnp.int32, totals.shape[2:], 0)

        def step(j, carry):
            cols = pl.ds(pl.multiple_of(j * width, 128), width)
            keys = kbuf[c, :, :, cols].reshape(n * prows, width)
            values = vbuf[c, :, :, cols].reshape(n * prows, width)
            kf = features(keys, fks[me * own + c * per + j], ones_blocks)
            kf = jnp.where(keep, kf.astype(F32), 0.0).astype(BF16)
            state[me, c, pl.ds(pl.multiple_of(j * width, 128), width), :] = dot(
                values.T, kf
            ).astype(BF16)
            total = dot(jnp.ones((totals.shape[2], n * prows), BF16), kf)
            return jnp.where(line == j, total, carry)

        found = lax.fori_loop(0, per, step, jnp.zeros(totals.shape[2:], F32))
        totals[me, c] = found.astype(BF16)
        for i in range(1, n):
            for copy in state_copies(c, i):
                copy.start()

    marks = [heads * 3 // 8 // 2 * 2, heads * 5 // 8 // 2 * 2]
    bounds = [0] + marks[:chunks] + [heads]
    for c in range(chunks):
        intra(bounds[c], bounds[c + 1])
        states(c)

    for i in range(1, n):
        for copy in info_copies(i):
            copy.wait_recv()
    total_reward = trew[0]
    for d in range(1, n):
        total_reward = total_reward + trew[d]
    mean = total_reward / n
    squares = jnp.zeros((8, 128), F32)
    for d in range(n):
        squares = squares + (trew[d] - mean) * (trew[d] - mean)
    gsum[grp] = squares
    table_copy = pltpu.make_async_copy(tinfo, tsm, sm_sem)
    table_copy.start()
    for i in range(1, groups):
        group_copy(i).start()

    intra(bounds[chunks], heads)
    table_copy.wait()

    piece_of = []
    for i in range(n):
        found = jnp.int32(0)
        for j in range(slot_count):
            ident = tsm[peer(i), 0, j] - me * pieces
            found = jnp.where((ident >= 0) & (ident < pieces), ident, found)
        piece_of.append(found)

    live = lax.broadcasted_iota(jnp.int32, (rows, width), 0) < rlen[0, 0]

    def combine_head(owner, c, j):
        h = owner * own + c * per + j
        tot = totals[owner, c].astype(F32)
        line = lax.broadcasted_iota(jnp.int32, tot.shape, 0)
        tot = jnp.sum(jnp.where(line == j, tot, 0.0), axis=0, keepdims=True)
        right = jnp.broadcast_to(tot, (width, tot.shape[1])).astype(BF16)
        part = state[owner, c, pl.ds(pl.multiple_of(j * width, 128), width), :]
        prompt = dot(phq[h], jnp.concatenate([part, right], axis=0), NT)
        both = prompt.astype(BF16).astype(F32) + inum[h]
        result = jnp.where(live, both[:, :width] / both[:, width:], 0.0)
        cols = pl.ds(pl.multiple_of(h * width, 128), width)
        for i in range(n):
            block = result[:BLK]
            for p in range(1, pieces):
                block = jnp.where(piece_of[i] == p, result[p * BLK : (p + 1) * BLK], block)
            if i == 0:
                orecv[me, :, cols] = block.astype(BF16)
            else:
                ostage[i - 1, :, cols] = block.astype(BF16)

    for step in range(n):
        owner = source(step)
        for c in range(chunks):
            if step > 0:
                for copy in state_copies(c, step):
                    copy.wait_recv()

            def body(j, carry, c=c, owner=owner):
                combine_head(owner, c, j)
                return carry

            lax.fori_loop(0, per, body, 0)
        for i in range(1, n):
            out_copy(step, i).start()

    for i in range(1, groups):
        group_copy(i).wait_recv()
    spread = gsum[0]
    for g in range(1, groups):
        spread = spread + gsum[g]
    scale = jnp.sqrt(spread / (groups * n) + 1e-06)
    adv = jnp.zeros((8, 128), F32)
    for j in range(slot_count):
        ident = slots_sm[0, j]
        src = lax.div(ident, pieces)
        start = lax.rem(ident, pieces) * BLK
        reward = jnp.zeros((8, 128), F32)
        size = jnp.int32(0)
        for d in range(n):
            reward = jnp.where(src == d, trew[d], reward)
            size = jnp.where(src == d, tsm[d, 0, slot_count], size)
        value = jnp.where(start + lane - j * BLK < size, (reward - mean) / scale, 0.0)
        adv = jnp.where((lane >= j * BLK) & (lane < (j + 1) * BLK), value, adv)
    adv_ref[...] = adv[:1]

    for step in range(n):
        for i in range(1, n):
            out_copy(step, i).wait_recv()
    for j in range(slot_count):
        src = lax.div(slots_sm[0, j], pieces)
        out_ref[0, j * BLK : (j + 1) * BLK, :] = orecv[src]

    for i in range(1, n):
        for copy in info_copies(i):
            copy.wait_send()
        for c in range(chunks):
            for copy in kv_copies(c, i) + state_copies(c, i):
                copy.wait_send()
        for step in range(n):
            out_copy(step, i).wait_send()
    for i in range(1, groups):
        group_copy(i).wait_send()


def body(
    resp_q, resp_k, resp_v, prompt_k, prompt_v, prompt_len, resp_len, assign, rewards,
    feat_q, feat_k,
):
    n = lax.axis_size("dp")
    groups = lax.axis_size("group")
    heads, width, feat = feat_q.shape
    rows = resp_q.shape[1]
    prows = prompt_k.shape[1]
    model = resp_q.shape[2]
    own = heads // n
    chunks = 2 if own % 2 == 0 else 1
    per = own // chunks
    slot_count = assign.shape[1]
    lines = -(-per // 16) * 16
    smem = pl.BlockSpec(memory_space=pltpu.SMEM)
    hbm = pl.BlockSpec(memory_space=pl.ANY)
    vmem = pl.BlockSpec(memory_space=pltpu.VMEM)
    dma = pltpu.SemaphoreType.DMA
    return pl.pallas_call(
        functools.partial(kernel, n, groups, heads, chunks),
        out_shape=(
            jax.ShapeDtypeStruct((1, slot_count * BLK, model), BF16),
            jax.ShapeDtypeStruct((1, slot_count * BLK), F32),
        ),
        in_specs=[smem] * 4 + [hbm] * 7,
        out_specs=(vmem, vmem),
        scratch_shapes=[
            pltpu.VMEM((rows, model), BF16),
            pltpu.VMEM((rows, model), BF16),
            pltpu.VMEM((rows, model), BF16),
            pltpu.VMEM((heads, width, feat), BF16),
            pltpu.VMEM((heads, width, feat), BF16),
            pltpu.VMEM((chunks, n, prows, per * width), BF16),
            pltpu.VMEM((chunks, n, prows, per * width), BF16),
            pltpu.VMEM((n, chunks, per * width, 2 * feat), BF16),
            pltpu.VMEM((n, chunks, lines, 2 * feat), BF16),
            pltpu.VMEM((heads, rows, 2 * feat), BF16),
            pltpu.VMEM((heads, rows, 2 * width), F32),
            pltpu.VMEM((n - 1, BLK, model), BF16),
            pltpu.VMEM((n, BLK, model), BF16),
            pltpu.VMEM((n, 8, 128), jnp.int32),
            pltpu.VMEM((n, 8, 128), F32),
            pltpu.SMEM((n, 8, 128), jnp.int32),
            pltpu.VMEM((groups, 8, 128), F32),
            dma((5,)),
            dma((chunks, 2)),
            dma((chunks, 2, n)),
            dma((chunks, 2, n)),
            dma((chunks, 2, n)),
            dma((chunks, 2, n)),
            dma((n, n)),
            dma((n, n)),
            dma((2, n)),
            dma((2, n)),
            dma((groups,)),
            dma((groups,)),
            dma,
        ],
        compiler_params=pltpu.CompilerParams(
            collective_id=0, has_side_effects=True, vmem_limit_bytes=62 * 1024 * 1024
        ),
        name="hedgehog",
    )(
        prompt_len, resp_len, assign, rewards, resp_q, resp_k, resp_v, prompt_k, prompt_v,
        feat_q, feat_k,
    )


def solution(mesh):
    return jax.shard_map(
        body,
        mesh=mesh,
        in_specs=(
            P("group", "dp", None),
            P("group", "dp", None),
            P("group", "dp", None),
            P("group", "dp", None),
            P("group", "dp", None),
            P("group"),
            P("group", "dp"),
            P("group", "dp"),
            P("group", "dp"),
            P(),
            P(),
        ),
        out_specs=(P("group", "dp", None), P("group", "dp")),
        check_vma=False,
    )
```

```python
import functools

import jax
import jax.numpy as jnp
from jax import lax
from jax.experimental import pallas as pl
from jax.experimental.pallas import tpu as pltpu
from jax.sharding import PartitionSpec as P

BLK = 64
MESH = pl.DeviceIdType.MESH
NT = (((1,), (1,)), ((), ()))
NN = (((1,), (0,)), ((), ()))
F32 = jnp.float32
BF16 = jnp.bfloat16


def dot(a, b, dims=NN):
    return lax.dot_general(a, b, dims, preferred_element_type=F32)


def features(rows, weights, ones_blocks):
    logits = dot(rows, weights)
    top = jnp.max(logits, axis=-1, keepdims=True)
    low = jnp.min(logits, axis=-1, keepdims=True)
    both = jnp.concatenate([jnp.exp(logits - top), jnp.exp(low - logits)], axis=1)
    sums = dot(both.astype(BF16), ones_blocks)
    return (both * (1.0 / sums)).astype(BF16)


def kernel(
    n, across, groups, heads, chunks,
    plen, rlen, slots_sm, rew_sm, q_hbm, k_hbm, v_hbm, pk_hbm, pv_hbm, fq_hbm, fk_hbm,
    orecv, adv_ref,
    qs, ks, vs, fqs, fks, kbuf, vbuf, state, phq, inum, ostage,
    tinfo, trew, tsm, gsum,
    load_sem, self_sem, oself_sem, kv_send, kv_recv, st_send, st_recv, o_send, o_recv,
    i_send, i_recv, g_send, g_recv, sm_sem,
):
    me = lax.axis_index("dp")
    grp = lax.axis_index("group")
    rows = qs.shape[0]
    width = fqs.shape[2]
    pieces = rows // BLK
    slot_count = slots_sm.shape[1]
    own = heads // n
    per = own // chunks
    prows = pk_hbm.shape[1]

    down = n // across
    row = me // across
    col = me % across

    def peer(i):
        return (row + i // across) % down * across + (col + i % across) % across

    def source(i):
        return (row + down - i // across) % down * across + (col + across - i % across) % across

    loads = [
        pltpu.make_async_copy(src, dst, load_sem.at[i])
        for i, (src, dst) in enumerate(
            [(fq_hbm, fqs), (fk_hbm, fks), (q_hbm.at[0], qs), (k_hbm.at[0], ks), (v_hbm.at[0], vs)]
        )
    ]

    lane = lax.broadcasted_iota(jnp.int32, (8, 128), 1)
    info = jnp.where(lane == slot_count, rlen[0, 0], 0)
    for j in range(slot_count):
        info = jnp.where(lane == j, slots_sm[0, j], info)
    tinfo[me] = info
    trew[me] = jnp.full((8, 128), rew_sm[0, 0], F32)

    barrier = pltpu.get_barrier_semaphore()
    for i in range(1, n):
        pl.semaphore_signal(barrier, inc=1, device_id={"dp": peer(i)}, device_id_type=MESH)
    for i in range(1, groups):
        pl.semaphore_signal(
            barrier, inc=1, device_id={"group": lax.rem(grp + i, groups)}, device_id_type=MESH
        )
    for copy in loads:
        copy.start()
    pl.semaphore_wait(barrier, n + groups - 2)

    def remote(src, dst, send, recv, axis, target):
        return pltpu.make_async_remote_copy(
            src_ref=src, dst_ref=dst, send_sem=send, recv_sem=recv,
            device_id={axis: target}, device_id_type=MESH,
        )

    def kv_cols(owner, c):
        return pl.ds(pl.multiple_of((owner * own + c * per) * width, 128), per * width)

    def kv_copies(c, i):
        result = []
        for a, (hbm, buf) in enumerate([(pk_hbm, kbuf), (pv_hbm, vbuf)]):
            src = hbm.at[0, :, kv_cols(peer(i), c)]
            dst = buf.at[c, me]
            if i == 0:
                result.append(pltpu.make_async_copy(src, dst, self_sem.at[c, a]))
            else:
                result.append(
                    remote(src, dst, kv_send.at[c, a, i], kv_recv.at[c, a, i], "dp", peer(i))
                )
        return result

    def info_copies(i):
        return [
            remote(tinfo.at[me], tinfo.at[me], i_send.at[0, i], i_recv.at[0, i], "dp", peer(i)),
            remote(trew.at[me], trew.at[me], i_send.at[1, i], i_recv.at[1, i], "dp", peer(i)),
        ]

    def group_copy(i):
        return remote(
            gsum.at[grp], gsum.at[grp], g_send.at[i], g_recv.at[i], "group",
            lax.rem(grp + i, groups),
        )

    def state_copy(c, i):
        dr, dc = i // across, i % across
        if c % 2 == 0:
            target, holder = (dr * across, dc) if dr else (dc, 0)
        else:
            target, holder = (dc, dr * across) if dc else (dr * across, 0)
        chunk = state.at[source(holder), c]
        return remote(chunk, chunk, st_send.at[c, i], st_recv.at[c, i], "dp", peer(target))

    straight = [i for i in range(1, n) if i < across or i % across == 0]
    relayed = [i for i in range(1, n) if i not in straight]

    def feeds(c):
        return [i for i in straight if (i < across if c % 2 == 0 else i % across == 0)]

    def relay(c):
        for i in feeds(c):
            state_copy(c, i).wait_recv()
        for i in relayed:
            state_copy(c, i).start()

    def out_cols(step):
        return pl.ds(pl.multiple_of(source(step) * own * width, 128), own * width)

    def out_copy(step, i):
        cols = out_cols(step)
        src, dst = ostage.at[i, :, cols], orecv.at[me, :, cols]
        if i == 0:
            return pltpu.make_async_copy(src, dst, oself_sem.at[step])
        return remote(src, dst, o_send.at[step, i], o_recv.at[step, i], "dp", peer(i))

    for i in range(1, n):
        for copy in info_copies(i):
            copy.start()
    for c in range(chunks):
        for i in [*range(1, n), 0]:
            for copy in kv_copies(c, i):
                copy.start()

    feat = fqs.shape[2]
    left = lax.broadcasted_iota(jnp.int32, (2 * feat, 2 * feat), 0) < feat
    upper = lax.broadcasted_iota(jnp.int32, (2 * feat, 2 * feat), 1) < feat
    ones_blocks = jnp.where(left == upper, 1.0, 0.0).astype(BF16)

    for copy in loads:
        copy.wait()

    def intra_head(h):
        cols = pl.ds(pl.multiple_of(h * width, 128), width)
        qf = features(qs[:, cols], fqs[h], ones_blocks)
        kf = features(ks[:, cols], fks[h], ones_blocks)
        phq[h] = qf
        scores = dot(qf, kf, NT)
        causal = lax.broadcasted_iota(jnp.int32, (rows, rows), 0) >= lax.broadcasted_iota(
            jnp.int32, (rows, rows), 1
        )
        weight = jnp.where(causal, scores, 0.0).astype(BF16)
        value = jnp.concatenate([vs[:, cols], jnp.ones((rows, width), BF16)], axis=1)
        inum[h] = dot(weight, value)

    def intra(first, last):
        def step(t, carry):
            intra_head(first + 2 * t)
            intra_head(first + 2 * t + 1)
            return carry

        lax.fori_loop(0, (last - first) // 2, step, 0)

    def states(c):
        for i in range(n):
            for copy in kv_copies(c, i):
                copy.wait() if i == 0 else copy.wait_recv()
        keep = lax.broadcasted_iota(jnp.int32, (n * prows, 2 * feat), 0) < plen[0]
        lines = (state.shape[2] - per * width, 2 * feat)
        line = lax.broadcasted_iota(jnp.int32, lines, 0)

        def step(j, carry):
            cols = pl.ds(pl.multiple_of(j * width, 128), width)
            keys = kbuf[c, :, :, cols].reshape(n * prows, width)
            values = vbuf[c, :, :, cols].reshape(n * prows, width)
            kf = features(keys, fks[me * own + c * per + j], ones_blocks)
            kf = jnp.where(keep, kf.astype(F32), 0.0).astype(BF16)
            state[me, c, pl.ds(pl.multiple_of(j * width, 128), width), :] = dot(
                values.T, kf
            ).astype(BF16)
            total = dot(jnp.ones((lines[0], n * prows), BF16), kf)
            return jnp.where(line == j, total, carry)

        found = lax.fori_loop(0, per, step, jnp.zeros(lines, F32))
        state[me, c, per * width :, :] = found.astype(BF16)
        for i in straight:
            state_copy(c, i).start()

    bounds = [heads * part // 32 * 2 for part in (0, 6, 9, 12)]
    for c in range(chunks):
        intra(bounds[c], bounds[c + 1])
        states(c)
    relay(0)
    if chunks > 1:
        intra(bounds[2], bounds[3])
        relay(1)

    for i in range(1, n):
        for copy in info_copies(i):
            copy.wait_recv()
    total_reward = trew[0]
    for d in range(1, n):
        total_reward = total_reward + trew[d]
    mean = total_reward / n
    squares = jnp.zeros((8, 128), F32)
    for d in range(n):
        squares = squares + (trew[d] - mean) * (trew[d] - mean)
    gsum[grp] = squares
    table_copy = pltpu.make_async_copy(tinfo, tsm, sm_sem)
    table_copy.start()
    for i in range(1, groups):
        group_copy(i).start()

    intra(bounds[3] if chunks > 1 else bounds[1], heads)
    table_copy.wait()

    piece_of = []
    for i in range(n):
        found = jnp.int32(0)
        for j in range(slot_count):
            ident = tsm[peer(i), 0, j] - me * pieces
            found = jnp.where((ident >= 0) & (ident < pieces), ident, found)
        piece_of.append(found)

    live = lax.broadcasted_iota(jnp.int32, (rows, width), 0) < rlen[0, 0]

    def combine_head(owner, c, j):
        h = owner * own + c * per + j
        tot = state[owner, c, per * width :, :].astype(F32)
        line = lax.broadcasted_iota(jnp.int32, tot.shape, 0)
        tot = jnp.sum(jnp.where(line == j, tot, 0.0), axis=0, keepdims=True)
        right = jnp.broadcast_to(tot, (width, tot.shape[1])).astype(BF16)
        part = state[owner, c, pl.ds(pl.multiple_of(j * width, 128), width), :]
        prompt = dot(phq[h], jnp.concatenate([part, right], axis=0), NT)
        both = prompt.astype(BF16).astype(F32) + inum[h]
        result = jnp.where(live, both[:, :width] / both[:, width:], 0.0)
        cols = pl.ds(pl.multiple_of(h * width, 128), width)
        for i in range(n):
            block = result[:BLK]
            for p in range(1, pieces):
                block = jnp.where(piece_of[i] == p, result[p * BLK : (p + 1) * BLK], block)
            ostage[i, :, cols] = block.astype(BF16)

    for step in range(n):
        owner = source(step)
        for c in range(chunks):
            if step > 0 and step not in feeds(c):
                state_copy(c, step).wait_recv()

            def body(j, carry, c=c, owner=owner):
                combine_head(owner, c, j)
                return carry

            lax.fori_loop(0, per, body, 0)
        for i in [*range(1, n), 0]:
            out_copy(step, i).start()

    for i in range(1, groups):
        group_copy(i).wait_recv()
    spread = gsum[0]
    for g in range(1, groups):
        spread = spread + gsum[g]
    scale = jnp.sqrt(spread / (groups * n) + 1e-06)
    adv = jnp.zeros((8, 128), F32)
    for j in range(slot_count):
        ident = slots_sm[0, j]
        src = lax.div(ident, pieces)
        start = lax.rem(ident, pieces) * BLK
        reward = jnp.zeros((8, 128), F32)
        size = jnp.int32(0)
        for d in range(n):
            reward = jnp.where(src == d, trew[d], reward)
            size = jnp.where(src == d, tsm[d, 0, slot_count], size)
        value = jnp.where(start + lane - j * BLK < size, (reward - mean) / scale, 0.0)
        adv = jnp.where((lane >= j * BLK) & (lane < (j + 1) * BLK), value, adv)
    adv_ref[...] = adv[:1]

    for step in range(n):
        for i in range(n):
            out_copy(step, i).wait_recv() if i else out_copy(step, i).wait()

    for i in range(1, n):
        for copy in info_copies(i):
            copy.wait_send()
        for c in range(chunks):
            for copy in kv_copies(c, i) + [state_copy(c, i)]:
                copy.wait_send()
        for step in range(n):
            out_copy(step, i).wait_send()
    for i in range(1, groups):
        group_copy(i).wait_send()


def pick(slots, block_ref, adv_ref, out_ref, adv_out_ref):
    out_ref[...] = block_ref[...]
    adv_out_ref[...] = adv_ref[...]


def body(
    resp_q, resp_k, resp_v, prompt_k, prompt_v, prompt_len, resp_len, assign, rewards,
    feat_q, feat_k,
):
    n = lax.axis_size("dp")
    groups = lax.axis_size("group")
    heads, width, feat = feat_q.shape
    rows = resp_q.shape[1]
    prows = prompt_k.shape[1]
    model = resp_q.shape[2]
    own = heads // n
    chunks = 2 if own % 2 == 0 else 1
    per = own // chunks
    slot_count = assign.shape[1]
    lines = -(-per // 16) * 16
    smem = pl.BlockSpec(memory_space=pltpu.SMEM)
    hbm = pl.BlockSpec(memory_space=pl.ANY)
    vmem = pl.BlockSpec(memory_space=pltpu.VMEM)
    dma = pltpu.SemaphoreType.DMA
    across = max(b for b in range(1, n + 1) if n % b == 0 and b * b <= n)
    arrived, adv = pl.pallas_call(
        functools.partial(kernel, n, across, groups, heads, chunks),
        out_shape=(
            jax.ShapeDtypeStruct((n, BLK, model), BF16),
            jax.ShapeDtypeStruct((1, slot_count * BLK), F32),
        ),
        in_specs=[smem] * 4 + [hbm] * 7,
        out_specs=(hbm, vmem),
        scratch_shapes=[
            pltpu.VMEM((rows, model), BF16),
            pltpu.VMEM((rows, model), BF16),
            pltpu.VMEM((rows, model), BF16),
            pltpu.VMEM((heads, width, feat), BF16),
            pltpu.VMEM((heads, width, feat), BF16),
            pltpu.VMEM((chunks, n, prows, per * width), BF16),
            pltpu.VMEM((chunks, n, prows, per * width), BF16),
            pltpu.VMEM((n, chunks, per * width + lines, 2 * feat), BF16),
            pltpu.VMEM((heads, rows, 2 * feat), BF16),
            pltpu.VMEM((heads, rows, 2 * width), F32),
            pltpu.VMEM((n, BLK, model), BF16),
            pltpu.VMEM((n, 8, 128), jnp.int32),
            pltpu.VMEM((n, 8, 128), F32),
            pltpu.SMEM((n, 8, 128), jnp.int32),
            pltpu.VMEM((groups, 8, 128), F32),
            dma((5,)),
            dma((chunks, 2)),
            dma((n,)),
            dma((chunks, 2, n)),
            dma((chunks, 2, n)),
            dma((chunks, n)),
            dma((chunks, n)),
            dma((n, n)),
            dma((n, n)),
            dma((2, n)),
            dma((2, n)),
            dma((groups,)),
            dma((groups,)),
            dma,
        ],
        compiler_params=pltpu.CompilerParams(
            collective_id=0, has_side_effects=True, vmem_limit_bytes=62 * 1024 * 1024
        ),
        name="hedgehog",
    )(
        prompt_len, resp_len, assign, rewards, resp_q, resp_k, resp_v, prompt_k, prompt_v,
        feat_q, feat_k,
    )

    pieces = rows // BLK
    return pl.pallas_call(
        pick,
        out_shape=(
            jax.ShapeDtypeStruct((1, slot_count * BLK, model), BF16),
            jax.ShapeDtypeStruct(adv.shape, F32),
        ),
        grid_spec=pltpu.PrefetchScalarGridSpec(
            num_scalar_prefetch=1,
            grid=(slot_count,),
            in_specs=[
                pl.BlockSpec((1, BLK, model), lambda j, slots: (lax.div(slots[0, j], pieces), 0, 0)),
                pl.BlockSpec(adv.shape, lambda j, slots: (0, 0)),
            ],
            out_specs=(
                pl.BlockSpec((1, BLK, model), lambda j, slots: (0, j, 0)),
                pl.BlockSpec(adv.shape, lambda j, slots: (0, 0)),
            ),
        ),
        name="pick",
    )(assign, arrived, adv)


def solution(mesh):
    return jax.shard_map(
        body,
        mesh=mesh,
        in_specs=(
            P("group", "dp", None),
            P("group", "dp", None),
            P("group", "dp", None),
            P("group", "dp", None),
            P("group", "dp", None),
            P("group"),
            P("group", "dp"),
            P("group", "dp"),
            P("group", "dp"),
            P(),
            P(),
        ),
        out_specs=(P("group", "dp", None), P("group", "dp")),
        check_vma=False,
    )
```

```python
import functools

import jax
import jax.numpy as jnp
from jax import lax
from jax.experimental import pallas as pl
from jax.experimental.pallas import tpu as pltpu
from jax.sharding import PartitionSpec as P

BLK = 64
MESH = pl.DeviceIdType.MESH
NT = (((1,), (1,)), ((), ()))
NN = (((1,), (0,)), ((), ()))
F32 = jnp.float32
BF16 = jnp.bfloat16


def dot(a, b, dims=NN):
    return lax.dot_general(a, b, dims, preferred_element_type=F32)


def features(rows, weights, ones_blocks):
    logits = dot(rows, weights)
    top = jnp.max(logits, axis=-1, keepdims=True)
    low = jnp.min(logits, axis=-1, keepdims=True)
    both = jnp.concatenate([jnp.exp(logits - top), jnp.exp(low - logits)], axis=1)
    sums = dot(both.astype(BF16), ones_blocks)
    return (both * (1.0 / sums)).astype(BF16)


def kernel(
    n, across, groups, heads, chunks,
    plen, rlen, slots_sm, rew_sm, q_hbm, k_hbm, v_hbm, pk_hbm, pv_hbm, fq_hbm, fk_hbm,
    orecv, adv_ref,
    qs, ks, vs, fqs, fks, kbuf, vbuf, state, phq, inum, ostage,
    tinfo, trew, tsm, gsum,
    load_sem, self_sem, oself_sem, kv_send, kv_recv, st_send, st_recv, o_send, o_recv,
    i_send, i_recv, g_send, g_recv, sm_sem,
):
    me = lax.axis_index("dp")
    grp = lax.axis_index("group")
    rows = qs.shape[0]
    width = fqs.shape[2]
    pieces = rows // BLK
    slot_count = slots_sm.shape[1]
    own = heads // n
    per = own // chunks
    prows = pk_hbm.shape[1]

    down = n // across
    row = me // across
    col = me % across

    def peer(i):
        return (row + i // across) % down * across + (col + i % across) % across

    def source(i):
        return (row + down - i // across) % down * across + (col + across - i % across) % across

    loads = [
        pltpu.make_async_copy(src, dst, load_sem.at[i])
        for i, (src, dst) in enumerate(
            [(fq_hbm, fqs), (fk_hbm, fks), (q_hbm.at[0], qs), (k_hbm.at[0], ks), (v_hbm.at[0], vs)]
        )
    ]

    lane = lax.broadcasted_iota(jnp.int32, (8, 128), 1)
    info = jnp.where(lane == slot_count, rlen[0, 0], 0)
    for j in range(slot_count):
        info = jnp.where(lane == j, slots_sm[0, j], info)
    tinfo[me] = info
    trew[me] = jnp.full((8, 128), rew_sm[0, 0], F32)

    barrier = pltpu.get_barrier_semaphore()
    for i in range(1, n):
        pl.semaphore_signal(barrier, inc=1, device_id={"dp": peer(i)}, device_id_type=MESH)
    for i in range(1, groups):
        pl.semaphore_signal(
            barrier, inc=1, device_id={"group": lax.rem(grp + i, groups)}, device_id_type=MESH
        )
    for copy in loads:
        copy.start()
    pl.semaphore_wait(barrier, n + groups - 2)

    def remote(src, dst, send, recv, axis, target):
        return pltpu.make_async_remote_copy(
            src_ref=src, dst_ref=dst, send_sem=send, recv_sem=recv,
            device_id={axis: target}, device_id_type=MESH,
        )

    def kv_cols(owner, c):
        return pl.ds(pl.multiple_of((owner * own + c * per) * width, 128), per * width)

    def kv_copies(c, i):
        result = []
        for a, (hbm, buf) in enumerate([(pk_hbm, kbuf), (pv_hbm, vbuf)]):
            src = hbm.at[0, :, kv_cols(peer(i), c)]
            dst = buf.at[c, me]
            if i == 0:
                result.append(pltpu.make_async_copy(src, dst, self_sem.at[c, a]))
            else:
                result.append(
                    remote(src, dst, kv_send.at[c, a, i], kv_recv.at[c, a, i], "dp", peer(i))
                )
        return result

    def info_copies(i):
        return [
            remote(tinfo.at[me], tinfo.at[me], i_send.at[0, i], i_recv.at[0, i], "dp", peer(i)),
            remote(trew.at[me], trew.at[me], i_send.at[1, i], i_recv.at[1, i], "dp", peer(i)),
        ]

    def group_copy(i):
        return remote(
            gsum.at[grp], gsum.at[grp], g_send.at[i], g_recv.at[i], "group",
            lax.rem(grp + i, groups),
        )

    def state_copy(c, i):
        dr, dc = i // across, i % across
        if c % 2 == 0:
            target, holder = (dr * across, dc) if dr else (dc, 0)
        else:
            target, holder = (dc, dr * across) if dc else (dr * across, 0)
        chunk = state.at[source(holder), c]
        return remote(chunk, chunk, st_send.at[c, i], st_recv.at[c, i], "dp", peer(target))

    straight = [i for i in range(1, n) if i < across or i % across == 0]
    relayed = [i for i in range(1, n) if i not in straight]

    def feeds(c):
        return [i for i in straight if (i < across if c % 2 == 0 else i % across == 0)]

    def relay(c):
        for i in feeds(c):
            state_copy(c, i).wait_recv()
        for i in relayed:
            state_copy(c, i).start()

    def out_cols(step):
        return pl.ds(pl.multiple_of(source(step) * own * width, 128), own * width)

    def out_copy(step, i):
        cols = out_cols(step)
        src, dst = ostage.at[i, :, cols], orecv.at[me, :, cols]
        if i == 0:
            return pltpu.make_async_copy(src, dst, oself_sem.at[step])
        return remote(src, dst, o_send.at[step, i], o_recv.at[step, i], "dp", peer(i))

    for i in range(1, n):
        for copy in info_copies(i):
            copy.start()
    for c in range(chunks):
        for i in [*range(1, n), 0]:
            for copy in kv_copies(c, i):
                copy.start()

    feat = fqs.shape[2]
    left = lax.broadcasted_iota(jnp.int32, (2 * feat, 2 * feat), 0) < feat
    upper = lax.broadcasted_iota(jnp.int32, (2 * feat, 2 * feat), 1) < feat
    ones_blocks = jnp.where(left == upper, 1.0, 0.0).astype(BF16)

    for copy in loads:
        copy.wait()

    def intra_head(h):
        cols = pl.ds(pl.multiple_of(h * width, 128), width)
        qf = features(qs[:, cols], fqs[h], ones_blocks)
        kf = features(ks[:, cols], fks[h], ones_blocks)
        phq[h] = qf
        scores = dot(qf, kf, NT)
        causal = lax.broadcasted_iota(jnp.int32, (rows, rows), 0) >= lax.broadcasted_iota(
            jnp.int32, (rows, rows), 1
        )
        weight = jnp.where(causal, scores, 0.0).astype(BF16)
        value = jnp.concatenate([vs[:, cols], jnp.ones((rows, width), BF16)], axis=1)
        inum[h] = dot(weight, value)

    def intra(first, last):
        def step(t, carry):
            intra_head(first + 2 * t)
            intra_head(first + 2 * t + 1)
            return carry

        lax.fori_loop(0, (last - first) // 2, step, 0)

    def states(c):
        for i in range(n):
            for copy in kv_copies(c, i):
                copy.wait() if i == 0 else copy.wait_recv()
        keep = lax.broadcasted_iota(jnp.int32, (n * prows, 2 * feat), 0) < plen[0]
        lines = (state.shape[2] - per * width, 2 * feat)
        line = lax.broadcasted_iota(jnp.int32, lines, 0)

        def step(j, carry):
            cols = pl.ds(pl.multiple_of(j * width, 128), width)
            keys = kbuf[c, :, :, cols].reshape(n * prows, width)
            values = vbuf[c, :, :, cols].reshape(n * prows, width)
            kf = features(keys, fks[me * own + c * per + j], ones_blocks)
            kf = jnp.where(keep, kf.astype(F32), 0.0).astype(BF16)
            state[me, c, pl.ds(pl.multiple_of(j * width, 128), width), :] = dot(
                values.T, kf
            ).astype(BF16)
            total = dot(jnp.ones((lines[0], n * prows), BF16), kf)
            return jnp.where(line == j, total, carry)

        found = lax.fori_loop(0, per, step, jnp.zeros(lines, F32))
        state[me, c, per * width :, :] = found.astype(BF16)
        for i in straight:
            state_copy(c, i).start()

    bounds = [heads * part // 32 * 2 for part in (0, 7, 11, 14)]
    for c in range(chunks):
        intra(bounds[c], bounds[c + 1])
        states(c)
    relay(0)
    if chunks > 1:
        intra(bounds[2], bounds[3])
        relay(1)

    for i in range(1, n):
        for copy in info_copies(i):
            copy.wait_recv()
    total_reward = trew[0]
    for d in range(1, n):
        total_reward = total_reward + trew[d]
    mean = total_reward / n
    squares = jnp.zeros((8, 128), F32)
    for d in range(n):
        squares = squares + (trew[d] - mean) * (trew[d] - mean)
    gsum[grp] = squares
    table_copy = pltpu.make_async_copy(tinfo, tsm, sm_sem)
    table_copy.start()
    for i in range(1, groups):
        group_copy(i).start()

    intra(bounds[3] if chunks > 1 else bounds[1], heads)
    table_copy.wait()

    piece_of = []
    for i in range(n):
        found = jnp.int32(0)
        for j in range(slot_count):
            ident = tsm[peer(i), 0, j] - me * pieces
            found = jnp.where((ident >= 0) & (ident < pieces), ident, found)
        piece_of.append(found)

    live = lax.broadcasted_iota(jnp.int32, (rows, width), 0) < rlen[0, 0]

    def combine_head(owner, c, j):
        h = owner * own + c * per + j
        tot = state[owner, c, per * width :, :].astype(F32)
        line = lax.broadcasted_iota(jnp.int32, tot.shape, 0)
        tot = jnp.sum(jnp.where(line == j, tot, 0.0), axis=0, keepdims=True)
        right = jnp.broadcast_to(tot, (width, tot.shape[1])).astype(BF16)
        part = state[owner, c, pl.ds(pl.multiple_of(j * width, 128), width), :]
        prompt = dot(phq[h], jnp.concatenate([part, right], axis=0), NT)
        both = prompt.astype(BF16).astype(F32) + inum[h]
        result = jnp.where(live, both[:, :width] / both[:, width:], 0.0)
        cols = pl.ds(pl.multiple_of(h * width, 128), width)
        for i in range(n):
            block = result[:BLK]
            for p in range(1, pieces):
                block = jnp.where(piece_of[i] == p, result[p * BLK : (p + 1) * BLK], block)
            ostage[i, :, cols] = block.astype(BF16)

    for step in range(n):
        owner = source(step)
        for c in range(chunks):
            if step > 0 and step not in feeds(c):
                state_copy(c, step).wait_recv()

            def body(j, carry, c=c, owner=owner):
                combine_head(owner, c, j)
                return carry

            lax.fori_loop(0, per, body, 0)
        for i in [*range(1, n), 0]:
            out_copy(step, i).start()

    for i in range(1, groups):
        group_copy(i).wait_recv()
    spread = gsum[0]
    for g in range(1, groups):
        spread = spread + gsum[g]
    scale = jnp.sqrt(spread / (groups * n) + 1e-06)
    adv = jnp.zeros((8, 128), F32)
    for j in range(slot_count):
        ident = slots_sm[0, j]
        src = lax.div(ident, pieces)
        start = lax.rem(ident, pieces) * BLK
        reward = jnp.zeros((8, 128), F32)
        size = jnp.int32(0)
        for d in range(n):
            reward = jnp.where(src == d, trew[d], reward)
            size = jnp.where(src == d, tsm[d, 0, slot_count], size)
        value = jnp.where(start + lane - j * BLK < size, (reward - mean) / scale, 0.0)
        adv = jnp.where((lane >= j * BLK) & (lane < (j + 1) * BLK), value, adv)
    adv_ref[...] = adv[:1]

    for step in range(n):
        for i in range(n):
            out_copy(step, i).wait_recv() if i else out_copy(step, i).wait()

    for i in range(1, n):
        for copy in info_copies(i):
            copy.wait_send()
        for c in range(chunks):
            for copy in kv_copies(c, i) + [state_copy(c, i)]:
                copy.wait_send()
        for step in range(n):
            out_copy(step, i).wait_send()
    for i in range(1, groups):
        group_copy(i).wait_send()


def pick(slots, block_ref, adv_ref, out_ref, adv_out_ref):
    out_ref[...] = block_ref[...]
    adv_out_ref[...] = adv_ref[...]


def body(
    resp_q, resp_k, resp_v, prompt_k, prompt_v, prompt_len, resp_len, assign, rewards,
    feat_q, feat_k,
):
    n = lax.axis_size("dp")
    groups = lax.axis_size("group")
    heads, width, feat = feat_q.shape
    rows = resp_q.shape[1]
    prows = prompt_k.shape[1]
    model = resp_q.shape[2]
    own = heads // n
    chunks = 2 if own % 2 == 0 else 1
    per = own // chunks
    slot_count = assign.shape[1]
    lines = -(-per // 16) * 16
    smem = pl.BlockSpec(memory_space=pltpu.SMEM)
    hbm = pl.BlockSpec(memory_space=pl.ANY)
    vmem = pl.BlockSpec(memory_space=pltpu.VMEM)
    dma = pltpu.SemaphoreType.DMA
    across = max(b for b in range(1, n + 1) if n % b == 0 and b * b <= n)
    arrived, adv = pl.pallas_call(
        functools.partial(kernel, n, across, groups, heads, chunks),
        out_shape=(
            jax.ShapeDtypeStruct((n, BLK, model), BF16),
            jax.ShapeDtypeStruct((1, slot_count * BLK), F32),
        ),
        in_specs=[smem] * 4 + [hbm] * 7,
        out_specs=(hbm, vmem),
        scratch_shapes=[
            pltpu.VMEM((rows, model), BF16),
            pltpu.VMEM((rows, model), BF16),
            pltpu.VMEM((rows, model), BF16),
            pltpu.VMEM((heads, width, feat), BF16),
            pltpu.VMEM((heads, width, feat), BF16),
            pltpu.VMEM((chunks, n, prows, per * width), BF16),
            pltpu.VMEM((chunks, n, prows, per * width), BF16),
            pltpu.VMEM((n, chunks, per * width + lines, 2 * feat), BF16),
            pltpu.VMEM((heads, rows, 2 * feat), BF16),
            pltpu.VMEM((heads, rows, 2 * width), F32),
            pltpu.VMEM((n, BLK, model), BF16),
            pltpu.VMEM((n, 8, 128), jnp.int32),
            pltpu.VMEM((n, 8, 128), F32),
            pltpu.SMEM((n, 8, 128), jnp.int32),
            pltpu.VMEM((groups, 8, 128), F32),
            dma((5,)),
            dma((chunks, 2)),
            dma((n,)),
            dma((chunks, 2, n)),
            dma((chunks, 2, n)),
            dma((chunks, n)),
            dma((chunks, n)),
            dma((n, n)),
            dma((n, n)),
            dma((2, n)),
            dma((2, n)),
            dma((groups,)),
            dma((groups,)),
            dma,
        ],
        compiler_params=pltpu.CompilerParams(
            collective_id=0, has_side_effects=True, vmem_limit_bytes=62 * 1024 * 1024
        ),
        name="hedgehog",
    )(
        prompt_len, resp_len, assign, rewards, resp_q, resp_k, resp_v, prompt_k, prompt_v,
        feat_q, feat_k,
    )

    pieces = rows // BLK
    return pl.pallas_call(
        pick,
        out_shape=(
            jax.ShapeDtypeStruct((1, slot_count * BLK, model), BF16),
            jax.ShapeDtypeStruct(adv.shape, F32),
        ),
        grid_spec=pltpu.PrefetchScalarGridSpec(
            num_scalar_prefetch=1,
            grid=(slot_count,),
            in_specs=[
                pl.BlockSpec((1, BLK, model), lambda j, slots: (lax.div(slots[0, j], pieces), 0, 0)),
                pl.BlockSpec(adv.shape, lambda j, slots: (0, 0)),
            ],
            out_specs=(
                pl.BlockSpec((1, BLK, model), lambda j, slots: (0, j, 0)),
                pl.BlockSpec(adv.shape, lambda j, slots: (0, 0)),
            ),
        ),
        name="pick",
    )(assign, arrived, adv)


def solution(mesh):
    return jax.shard_map(
        body,
        mesh=mesh,
        in_specs=(
            P("group", "dp", None),
            P("group", "dp", None),
            P("group", "dp", None),
            P("group", "dp", None),
            P("group", "dp", None),
            P("group"),
            P("group", "dp"),
            P("group", "dp"),
            P("group", "dp"),
            P(),
            P(),
        ),
        out_specs=(P("group", "dp", None), P("group", "dp")),
        check_vma=False,
    )
```
